256 devices in a mesh: blk: 8 (over z_lo, core), wide: 32 (over x, z_hi, y).
Axes of the slice: x: 4, y: 4, z: 8 (z_hi: 2, z_lo: 4; z = z_hi * 4 + z_lo), core: 2. Of those that a mesh axis runs over, the one named last changes fastest.
Arguments:
- surf_xyz: float32 [3, 131072], P(None, ('blk', 'wide')), may hold values from -5 to 5
- surf_disp: float32 [24, 131072], P(None, ('blk', 'wide')), may hold values from -12 to 12
- neighbours: int32 [4, 131072], P(None, ('blk', 'wide')), may hold values from 0 to 16383, as said below
- vol_xyz: float32 [3, 65536], P(None, ('blk', 'wide')), may hold values from -4 to 4
Outputs:
- displacement: float32 [24, 65536], P(None, ('blk', 'wide'))
The draws below stay inside these ranges and needn't reach their ends.
Inputs may be any that keep to these rules, and one draw needn't show every extreme that they name: `neighbours`: column j names surface nodes of the same group of 16384 consecutive nodes as j, by their index within that group; every group is a renumbering of square patches of 16 x 16 nodes.
All inputs are finite; a program needn't handle non-finite values.
Results may differ from the reference program's by a relative error of at most 0.012.
The reference program's roundings to bfloat16 on the way (of `blocks` and `weights`) count: a program that leaves them out, or rounds other values in their place, can miss the bound.
Values may be sent and summed in bfloat16 or wider, within the bound.
A program may use at most 64 MiB of HBM per device.

```python
import math
import jax
import jax.numpy as jnp
from jax import lax

CASES = 8
SIDE = 16
S_GRP = 16384
NSURF = 131072
NVOL = 65536


def node_order(key):
    groups = NSURF // S_GRP
    keys = jax.random.split(jax.random.fold_in(key, 7), groups)
    return jax.vmap(lambda one_key: jax.random.permutation(one_key, S_GRP))(keys).astype(jnp.int32)


def draw_neighbours(key, part):
    order = node_order(key)
    slots = jnp.arange(S_GRP, dtype=jnp.int32)
    area = SIDE * SIDE
    patch = slots // area
    row_pos = slots % area // SIDE
    col_pos = slots % SIDE
    base = patch * area
    targets = [base + row_pos * SIDE + jnp.minimum(col_pos + 1, SIDE - 1), base + row_pos * SIDE + jnp.maximum(col_pos - 1, 0), base + jnp.minimum(row_pos + 1, SIDE - 1) * SIDE + col_pos, base + jnp.maximum(row_pos - 1, 0) * SIDE + col_pos]

    def one_group(perm):
        rows = [jnp.zeros((S_GRP,), jnp.int32).at[perm].set(perm[target]) for target in targets]
        return jnp.stack(rows)
    table = jax.vmap(one_group)(order)
    return table.transpose(1, 0, 2).reshape(4, NSURF).astype(jnp.int32)


def draw_surf_xyz(key, part):
    order = node_order(key)
    groups = NSURF // S_GRP
    area = SIDE * SIDE
    patches = S_GRP // area
    key_one, key_two, key_three = jax.random.split(jax.random.fold_in(key, 11), 3)
    anchor = jnp.clip(jax.random.normal(key_one, (groups, patches, 3), jnp.float32), -3.0, 3.0)
    frame = jax.random.normal(key_two, (groups, patches, 2, 3), jnp.float32)
    frame = frame / jnp.sqrt(jnp.sum(frame * frame, axis=-1, keepdims=True) + 0.1)
    slots = jnp.arange(S_GRP, dtype=jnp.int32)
    patch = slots // area
    row_pos = (slots % area // SIDE).astype(jnp.float32) - SIDE / 2.0
    col_pos = (slots % SIDE).astype(jnp.float32) - SIDE / 2.0
    jitter = jnp.clip(jax.random.normal(key_three, (groups, S_GRP, 3), jnp.float32), -4.0, 4.0) * 0.01
    spot = anchor[:, patch] + 0.05 * col_pos[None, :, None] * frame[:, patch, 0] + 0.05 * row_pos[None, :, None] * frame[:, patch, 1] + jitter

    def one_group(perm, values):
        return jnp.zeros((S_GRP, 3), jnp.float32).at[perm].set(values)
    placed = jax.vmap(one_group)(order, spot)
    return placed.reshape(NSURF, 3).T.astype(jnp.float32)


def levels(key, extent, shards, least, largest):
    gain, own = 1.0, jax.random.fold_in(key, 6)
    for position, parts in shards:
        draws = jnp.exp(jax.random.uniform(jax.random.fold_in(own, position), (parts,), jnp.float32, least / len(shards), largest / len(shards)))
        gain = gain * jnp.repeat(draws, extent[position] // parts).reshape([-1 if axis == position else 1 for axis in range(len(extent))])
    return gain


def gaussian(stream_key, shape, deviation, reach, cuts=(), kind=jnp.bfloat16):
    loudness = levels(stream_key, shape, cuts, -0.22, 0.18) if cuts else 1.0
    entries = jax.random.normal(stream_key, shape, jnp.float32) * deviation * loudness
    return jnp.minimum(jnp.maximum(entries, -reach), reach).astype(kind)


def setup_inputs(seed: int = 0) -> dict:
    key_list = jax.random.split(jax.random.key(seed), 5)
    return {
        "surf_xyz": draw_surf_xyz(jax.random.fold_in(key_list[4], 71), 0),
        "surf_disp": gaussian(key_list[1], (3 * CASES, NSURF), 2.0, 12.0, ((1, 256),), jnp.float32),
        "neighbours": draw_neighbours(jax.random.fold_in(key_list[4], 71), 0),
        "vol_xyz": gaussian(key_list[3], (3, NVOL), 1.0, 4.0, ((1, 256),), jnp.float32),
    }


tangent_floor = 0.04
core_radius = 0.04


def form_blocks(source_xyz, source_disp, links, node_xyz, node_disp):
    count = links.shape[1]
    cases = node_disp.shape[0] // 3
    tangent_one = jnp.take(source_xyz, links[0], axis=1) - jnp.take(source_xyz, links[1], axis=1)
    tangent_two = jnp.take(source_xyz, links[2], axis=1) - jnp.take(source_xyz, links[3], axis=1)
    change_one = (jnp.take(source_disp, links[0], axis=1) - jnp.take(source_disp, links[1], axis=1)).reshape(cases, 3, count)
    change_two = (jnp.take(source_disp, links[2], axis=1) - jnp.take(source_disp, links[3], axis=1)).reshape(cases, 3, count)
    length_one = (tangent_one[0] * tangent_one[0] + tangent_one[1] * tangent_one[1]) + tangent_one[2] * tangent_one[2]
    length_two = (tangent_two[0] * tangent_two[0] + tangent_two[1] * tangent_two[1]) + tangent_two[2] * tangent_two[2]
    scaled_one = tangent_one / (length_one + tangent_floor)
    scaled_two = tangent_two / (length_two + tangent_floor)
    linear = change_one[:, :, None, :] * scaled_one[None, None, :, :] + change_two[:, :, None, :] * scaled_two[None, None, :, :]
    moved = node_disp.reshape(cases, 3, count)
    offset = (linear[:, :, 0, :] * node_xyz[0] + linear[:, :, 1, :] * node_xyz[1]) + linear[:, :, 2, :] * node_xyz[2]
    blocks = jnp.concatenate([linear.reshape(cases, 9, count), moved - offset], axis=1)
    return blocks.reshape(cases * 12, count).astype(jnp.bfloat16)


def pair_weights(source_xyz, target_xyz):
    delta_x = source_xyz[0][:, None] - target_xyz[0][None, :]
    delta_y = source_xyz[1][:, None] - target_xyz[1][None, :]
    delta_z = source_xyz[2][:, None] - target_xyz[2][None, :]
    radius = (delta_x * delta_x + delta_y * delta_y) + delta_z * delta_z + core_radius
    return (1.0 / (radius * radius)).astype(jnp.bfloat16)


def finish(numerator, denominator, target_xyz):
    cases = numerator.shape[0] // 12
    count = numerator.shape[1]
    grouped = numerator.reshape(cases, 12, count)
    linear = grouped[:, :9].reshape(cases, 3, 3, count)
    moved = ((linear[:, :, 0] * target_xyz[0] + linear[:, :, 1] * target_xyz[1]) + linear[:, :, 2] * target_xyz[2]) + grouped[:, 9:]
    return (moved / denominator).reshape(cases * 3, count)


def reference(surf_xyz, surf_disp, neighbours, vol_xyz):
    offsets = (jnp.arange(NSURF, dtype=jnp.int32) // S_GRP) * S_GRP
    links = (neighbours + offsets[None, :]).astype(jnp.int32)
    blocks = form_blocks(surf_xyz, surf_disp, links, surf_xyz, surf_disp)
    width = math.gcd(256, NVOL)
    batches = vol_xyz.reshape(3, NVOL // width, width).transpose(1, 0, 2)

    def one_batch(target_xyz):
        weights = pair_weights(surf_xyz, target_xyz)
        numerator = jnp.dot(blocks, weights, preferred_element_type=jnp.float32)
        denominator = jnp.sum(weights.astype(jnp.float32), axis=0)
        return finish(numerator, denominator, target_xyz)

    result = lax.map(one_batch, batches)
    return result.transpose(1, 0, 2).reshape(3 * CASES, NVOL)
```

```python
import jax
import jax.numpy as jnp
from jax import lax
from jax.experimental import pallas as pl
from jax.experimental.pallas import tpu as pltpu
from jax.sharding import PartitionSpec as P

MESH = pl.DeviceIdType.MESH
tangent_floor = 0.04
core_radius = 0.04
f32, bf16, i32 = jnp.float32, jnp.bfloat16, jnp.int32

NX, NY, NZ = 4, 4, 8
LOW = 4
OWN = 512
VOWN = 256
TILE = 512
SET = 8
S_ALL = SET * OWN
V_SLOTS = NX * NZ
V_ALL = V_SLOTS * VOWN
PER_TILE = TILE // VOWN
TILES = V_ALL // TILE
ROWS = 104
FEAT = 32
CACHED = 0


def device(x, y, z, core):
    return (lax.rem(z, LOW) * 2 + core, (x * 2 + lax.div(z, LOW)) * NY + y)


def offsets(slot):
    p, q = slot // NX, slot % NX
    dz = 4 + (1 - 2 * (p % 2)) * ((p + 1) // 2)
    dx = 2 + (1 - 2 * (q % 2)) * ((q + 1) // 2)
    return dx, dz


INVERSE = []
for slot in range(V_SLOTS):
    dx, dz = offsets(slot)
    INVERSE.append(
        [k for k in range(V_SLOTS) if offsets(k) == ((-dx) % NX, (-dz) % NZ)][0]
    )


def split(value):
    high = value.astype(bf16).astype(f32)
    rest = value - high
    middle = rest.astype(bf16).astype(f32)
    return high, middle, (rest - middle).astype(bf16).astype(f32)


PAIRS = ((0, 0), (0, 1), (1, 0), (0, 2), (2, 0), (1, 1), (1, 2), (2, 1))


def feature_rows(xyz, surface):
    count = xyz.shape[1]
    ones = jnp.ones((1, count), f32)
    rows = []
    scale = 1.0 if surface else -2.0
    norm = (xyz[0:1] * xyz[0:1] + xyz[1:2] * xyz[1:2]) + xyz[2:3] * xyz[2:3]
    for axis in range(3):
        parts = split(xyz[axis : axis + 1] * scale)
        rows += [parts[pair[0] if surface else pair[1]] for pair in PAIRS]
    if surface:
        rows += list(split(norm + core_radius)) + [ones] * 3
    else:
        rows += [ones] * 3 + list(split(norm))
    rows += [jnp.zeros((1, count), f32)] * (FEAT - len(rows))
    return jnp.concatenate(rows, axis=0)


def kernel(
    xyz_ref, disp_ref, near_ref, vol_ref, out_ref,
    tab, own_xyz, set_xyz, own_vol, vols, fs, fv, picked, near_rows, near_smem,
    own_blk, blk, part, got, cache,
    z_send, z_recv, x_send, y_send, chunk_recv, sx_send, sx_recv, v_send, v_recv,
    b_send, b_recv, r_send, r_recv, local_sem,
):
    blk_id, wide_id = lax.axis_index("blk"), lax.axis_index("wide")
    core = lax.rem(blk_id, 2)
    z_low = lax.div(blk_id, 2)
    y = lax.rem(wide_id, NY)
    z_high = lax.rem(lax.div(wide_id, NY), 2)
    x = lax.div(wide_id, NY * 2)
    z = z_high * LOW + z_low
    other = 1 - core
    wide_at = lambda ax, ah, ay: (ax * 2 + ah) * NY + ay
    xs = [lax.rem(x + d, NX) for d in range(NX)]
    ys = [lax.rem(y + d, NY) for d in range(NY)]
    far_z = lax.rem(z + LOW, NZ)
    far_h = 1 - z_high

    barrier = pltpu.get_barrier_semaphore()
    peers = []
    for slot in range(V_SLOTS - 1):
        dx, dz = offsets(slot)
        peers.append(device(lax.rem(x + dx, NX), y, lax.rem(z + dz, NZ), core))
    for d in range(1, NY):
        peers.append(device(x, ys[d], z, core))
    for d in range(NY):
        peers.append(device(x, ys[d], z, other))
    for peer in peers:
        pl.semaphore_signal(barrier, inc=1, device_id=peer, device_id_type=MESH)

    xyz = xyz_ref[...]
    disp = disp_ref[...]
    zeros5 = jnp.zeros((5, OWN), f32)
    table = jnp.concatenate([disp, xyz, zeros5], axis=0)
    stacked = jnp.concatenate(
        [table[:, q * 128 : (q + 1) * 128] for q in range(4)], axis=0
    )
    tab[wide_id] = stacked.T
    own_xyz[0:3, :] = xyz
    own_vol[0:3, :] = vol_ref[...]
    near = near_ref[...]
    near_rows[...] = (near // OWN) * 128 + (near & 127)
    to_smem = pltpu.make_async_copy(near_rows, near_smem, local_sem)

    pl.semaphore_wait(barrier, len(peers))
    to_smem.start()

    pending = []

    def send(src, dst, send_sem, recv_sem, peer):
        copy = pltpu.make_async_remote_copy(
            src_ref=src, dst_ref=dst, send_sem=send_sem, recv_sem=recv_sem,
            device_id=peer, device_id_type=MESH,
        )
        copy.start()
        pending.append(copy)

    half = lambda w, h: tab.at[w, pl.ds(h * 64, 64), :]

    def landed(ref, sem):
        pltpu.make_async_copy(ref, ref, sem).wait()

    def send_x(w, h, number):
        for d in range(1, NX):
            send(half(w, h), half(w, h), x_send.at[number, d], chunk_recv.at[w, h],
                 device(xs[d], y, z, core))

    def send_y(w, h, number):
        for d in range(1, NY):
            send(half(w, h), half(w, h), y_send.at[number, d], chunk_recv.at[w, h],
                 device(x, ys[d], z, core))

    far_peer = device(x, y, far_z, core)
    for h in range(2):
        send(half(wide_id, h), half(wide_id, h), z_send.at[h],
             chunk_recv.at[wide_id, h], far_peer)
    send_x(wide_id, 0, 0)
    send_y(wide_id, 1, 0)
    member = core * NY + y
    for c in range(2):
        for d in range(NY):
            if c == 0 and d == 0:
                continue
            send(own_xyz, set_xyz.at[member], sx_send.at[c, d], sx_recv.at[member],
                 device(x, ys[d], z, core if c == 0 else other))
    for slot in range(V_SLOTS - 1):
        dx, dz = offsets(slot)
        send(own_vol, vols.at[INVERSE[slot]], v_send.at[slot],
             v_recv.at[INVERSE[slot]],
             device(lax.rem(x + dx, NX), y, lax.rem(z + dz, NZ), core))

    far_w = wide_at(x, far_h, y)
    for h in range(2):
        landed(half(far_w, h), chunk_recv.at[far_w, h])
    send_x(far_w, 0, 1)
    send_y(far_w, 1, 1)
    number_a = number_b = 0
    send_y(wide_id, 0, 2)
    send_y(far_w, 0, 3)
    send_x(wide_id, 1, 2)
    send_x(far_w, 1, 3)
    number = 4
    for d in range(1, NX):
        for high in (z_high, far_h):
            w = wide_at(xs[d], high, y)
            landed(half(w, 0), chunk_recv.at[w, 0])
            send_y(w, 0, number)
            w = wide_at(x, high, ys[d])
            landed(half(w, 1), chunk_recv.at[w, 1])
            send_x(w, 1, number)
            number += 1

    set_xyz[member] = own_xyz[...]
    vols[V_SLOTS - 1] = own_vol[...]
    for c in range(2):
        for d in range(NY):
            who = (core if c == 0 else other) * NY + ys[d]
            if c or d:
                landed(set_xyz.at[who], sx_recv.at[who])
            rows = feature_rows(set_xyz[who], True)
            at = pl.multiple_of(who * OWN, OWN)
            fs[pl.ds(at, OWN), :] = rows.T.astype(bf16)
    for slot in range(V_SLOTS):
        if slot < V_SLOTS - 1:
            landed(vols.at[slot], v_recv.at[slot])
        fv[:, slot * VOWN : (slot + 1) * VOWN] = feature_rows(
            vols[slot], False
        ).astype(bf16)

    for d in range(1, NX):
        for e in range(1, NY):
            for high in (z_high, far_h):
                w = wide_at(xs[d], high, ys[e])
                for h in range(2):
                    landed(half(w, h), chunk_recv.at[w, h])
    for d in range(1, NX):
        for high in (z_high, far_h):
            w = wide_at(xs[d], high, y)
            landed(half(w, 1), chunk_recv.at[w, 1])
            w = wide_at(x, high, ys[d])
            landed(half(w, 0), chunk_recv.at[w, 0])

    to_smem.wait()
    STEP = 8

    def pick(group, _):
        for k in range(STEP):
            j = group * STEP + k
            for n in range(4):
                row = near_smem[n, j]
                picked[n, pl.ds(j, 1), :] = tab[lax.div(row, 128), pl.ds(lax.rem(row, 128), 1), :]
        return 0

    lax.fori_loop(0, OWN // STEP, pick, 0)
    chosen = []
    for n in range(4):
        quarter = lax.rem(lax.div(near[n : n + 1], 128), 4)
        turned = picked[n].T
        value = turned[0:32]
        for q in range(1, 4):
            value = jnp.where(quarter == q, turned[q * 32 : (q + 1) * 32], value)
        chosen.append(value)
    first, second = chosen[0] - chosen[1], chosen[2] - chosen[3]

    def scaled(change):
        t = change[24:27]
        length = (t[0:1] * t[0:1] + t[1:2] * t[1:2]) + t[2:3] * t[2:3]
        return t / (length + tangent_floor)

    one, two = scaled(first), scaled(second)
    linear = [
        first[0:24] * one[q : q + 1] + second[0:24] * two[q : q + 1] for q in range(3)
    ]
    offset = (linear[0] * xyz[0:1] + linear[1] * xyz[1:2]) + linear[2] * xyz[2:3]
    tail = jnp.where(lax.broadcasted_iota(i32, (8, OWN), 0) == 0, 1.0, 0.0)
    own_blk[...] = jnp.concatenate(linear + [disp - offset, tail], axis=0).astype(bf16)

    def columns(who):
        return blk.at[:, pl.ds(pl.multiple_of(who * OWN, OWN), OWN)]

    own_copy = pltpu.make_async_copy(own_blk, columns(member), local_sem)
    own_copy.start()
    for d in range(1, NY):
        send(own_blk, columns(member), b_send.at[d], b_recv.at[member],
             device(x, ys[d], z, core))
    send(own_blk, columns(member), b_send.at[0], b_recv.at[member],
         device(x, y, z, other))
    own_copy.wait()
    for d in (1, 3, 2):
        who = core * NY + ys[d]
        landed(columns(who), b_recv.at[who])
        send(columns(who), columns(who), b_send.at[3 + d], b_recv.at[who],
             device(x, y, z, other))
    for d in range(NY):
        who = other * NY + ys[d]
        landed(columns(who), b_recv.at[who])

    def weights(tile):
        at = pl.multiple_of(tile * TILE, TILE)
        radius = jnp.dot(fs[...], fv[:, pl.ds(at, TILE)], preferred_element_type=f32)
        return (1.0 / (radius * radius)).astype(bf16)

    def reduce_copy(slot):
        p, q = lax.div(slot, NX), lax.rem(slot, NX)
        dz = 4 + (1 - 2 * lax.rem(p, 2)) * lax.div(p + 1, 2)
        dx = 2 + (1 - 2 * lax.rem(q, 2)) * lax.div(q + 1, 2)
        ip = jnp.where((p == 0) | (p == 7), p, p + 2 * lax.rem(p, 2) - 1)
        iq = jnp.where((q == 0) | (q == 3), q, q + 2 * lax.rem(q, 2) - 1)
        there = ip * NX + iq
        return pltpu.make_async_remote_copy(
            src_ref=part.at[slot], dst_ref=got.at[there],
            send_sem=r_send.at[slot], recv_sem=r_recv.at[there],
            device_id=device(lax.rem(x + dx, NX), y, lax.rem(z + dz, NZ), core),
            device_id_type=MESH,
        )

    def finish_tile(tile, total):
        for k in range(PER_TILE):
            slot = tile * PER_TILE + k
            block = total[:, k * VOWN : (k + 1) * VOWN]
            at = vols[slot]
            moved = (
                (block[0:24] * at[0:1] + block[24:48] * at[1:2]) + block[48:72] * at[2:3]
            ) + block[72:96]
            part[slot] = jnp.concatenate([moved, block[96:104]], axis=0)

    def one_tile(tile, _):
        @pl.when(tile > 0)
        def _():
            for k in range(PER_TILE):
                reduce_copy((tile - 1) * PER_TILE + k).start()

        total = jnp.dot(blk[...], weights(tile), preferred_element_type=f32)
        finish_tile(tile, total)
        return 0

    lax.fori_loop(0, TILES, one_tile, 0)
    for k in range(PER_TILE - 1):
        reduce_copy((TILES - 1) * PER_TILE + k).start()

    total = part[V_SLOTS - 1]
    for slot in range(V_SLOTS - 1):
        landed(got.at[slot], r_recv.at[slot])
        total = total + got[slot]
    out_ref[...] = total[0:24] / total[24:25]

    for copy in pending:
        copy.wait_send()

    def sent(slot, _):
        reduce_copy(slot).wait_send()
        return 0

    lax.fori_loop(0, V_SLOTS - 1, sent, 0)


def on_device(surf_xyz, surf_disp, neighbours, vol_xyz):
    dma = pltpu.SemaphoreType.DMA
    vmem = pl.BlockSpec(memory_space=pltpu.VMEM)
    return pl.pallas_call(
        kernel,
        out_shape=jax.ShapeDtypeStruct((24, VOWN), f32),
        in_specs=[vmem] * 4,
        out_specs=vmem,
        scratch_shapes=[
            pltpu.VMEM((32, 128, 128), f32),
            pltpu.VMEM((8, OWN), f32),
            pltpu.VMEM((SET, 8, OWN), f32),
            pltpu.VMEM((8, VOWN), f32),
            pltpu.VMEM((V_SLOTS, 8, VOWN), f32),
            pltpu.VMEM((S_ALL, FEAT), bf16),
            pltpu.VMEM((FEAT, V_ALL), bf16),
            pltpu.VMEM((4, OWN, 128), f32),
            pltpu.VMEM((4, OWN), i32),
            pltpu.SMEM((4, OWN), i32),
            pltpu.VMEM((ROWS, OWN), bf16),
            pltpu.VMEM((ROWS, S_ALL), bf16),
            pltpu.VMEM((V_SLOTS, 32, VOWN), f32),
            pltpu.VMEM((V_SLOTS, 32, VOWN), f32),
            pltpu.VMEM((max(CACHED, 1), 8, 128) if not CACHED else (CACHED, S_ALL, TILE), bf16),
            dma((2,)), dma((2,)), dma((10, NX)), dma((10, NY)), dma((32, 2)),
            dma((2, NY)), dma((SET,)), dma((V_SLOTS,)), dma((V_SLOTS,)),
            dma((8,)), dma((SET,)), dma((V_SLOTS,)), dma((V_SLOTS,)), dma,
        ],
        compiler_params=pltpu.CompilerParams(
            collective_id=0, has_side_effects=True, vmem_limit_bytes=62 << 20
        ),
        name="warp",
    )(surf_xyz, surf_disp, neighbours, vol_xyz)


def solution(mesh):
    spec = P(None, ("blk", "wide"))
    return jax.shard_map(
        on_device, mesh=mesh, in_specs=(spec,) * 4, out_specs=spec, check_vma=False
    )
```

```python
import jax
import jax.numpy as jnp
from jax import lax
from jax.experimental import pallas as pl
from jax.experimental.pallas import tpu as pltpu
from jax.sharding import PartitionSpec as P

MESH = pl.DeviceIdType.MESH
tangent_floor = 0.04
core_radius = 0.04
f32, bf16, i32 = jnp.float32, jnp.bfloat16, jnp.int32

NX, NY, NZ = 4, 4, 8
LOW = 4
OWN = 512
VOWN = 256
TILE = 512
SET = 8
S_ALL = SET * OWN
V_SLOTS = NX * NZ
V_ALL = V_SLOTS * VOWN
PER_TILE = TILE // VOWN
TILES = V_ALL // TILE
ROWS = 104
FEAT = 32
CACHED = 12
EARLY = 8
RELAY_AT = (0, 1, 3)
BLOCKS_AT = 10
LAG = 3


def device(x, y, z, core):
    return (lax.rem(z, LOW) * 2 + core, (x * 2 + lax.div(z, LOW)) * NY + y)


def z_offset(p):
    if isinstance(p, int):
        return 4 + (1 - 2 * (p % 2)) * ((p + 1) // 2)
    return 4 + (1 - 2 * lax.rem(p, 2)) * lax.div(p + 1, 2)


def split(value):
    high = value.astype(bf16).astype(f32)
    rest = value - high
    middle = rest.astype(bf16).astype(f32)
    return high, middle, (rest - middle).astype(bf16).astype(f32)


PAIRS = ((0, 0), (0, 1), (1, 0), (0, 2), (2, 0), (1, 1), (1, 2), (2, 1))


def feature_rows(xyz, surface):
    count = xyz.shape[1]
    ones = jnp.ones((1, count), f32)
    rows = []
    scale = 1.0 if surface else -2.0
    norm = (xyz[0:1] * xyz[0:1] + xyz[1:2] * xyz[1:2]) + xyz[2:3] * xyz[2:3]
    for axis in range(3):
        parts = split(xyz[axis : axis + 1] * scale)
        rows += [parts[pair[0] if surface else pair[1]] for pair in PAIRS]
    if surface:
        rows += list(split(norm + core_radius)) + [ones] * 3
    else:
        rows += [ones] * 3 + list(split(norm))
    rows += [jnp.zeros((1, count), f32)] * (FEAT - len(rows))
    return jnp.concatenate(rows, axis=0)


def kernel(
    xyz_ref, disp_ref, near_ref, vol_ref, out_ref,
    tab, own_xyz, set_xyz, vols, fs, fv, picked, near_rows, near_smem,
    own_blk, blk, part, got_x, mid, got_z, cache,
    z_send, x_send, y_send, chunk_recv, sx_send, sx_recv, vx_send, vx_recv,
    vz_send, vz_recv, b_send, b_recv, rx_send, rx_recv, rz_send, rz_recv, local_sem,
):
    blk_id, wide_id = lax.axis_index("blk"), lax.axis_index("wide")
    core = lax.rem(blk_id, 2)
    z_low = lax.div(blk_id, 2)
    y = lax.rem(wide_id, NY)
    z_high = lax.rem(lax.div(wide_id, NY), 2)
    x = lax.div(wide_id, NY * 2)
    z = z_high * LOW + z_low
    other = 1 - core
    wide_at = lambda ax, ah, ay: (ax * 2 + ah) * NY + ay
    xs = [lax.rem(x + d, NX) for d in range(NX)]
    ys = [lax.rem(y + d, NY) for d in range(NY)]
    zs = [lax.rem(z + d, NZ) for d in range(NZ)]
    far_h = 1 - z_high
    x_peer = lambda d: device(xs[d], y, z, core)
    y_peer = lambda d: device(x, ys[d], z, core)
    z_peer = lambda d: device(x, y, zs[d], core)

    barrier = pltpu.get_barrier_semaphore()
    peers = [z_peer(4)] + [x_peer(d) for d in range(1, NX)]
    peers += [y_peer(d) for d in range(1, NY)]
    peers += [z_peer(d) for d in (3, 5, 2, 6, 1, 7)]
    peers += [device(x, ys[d], z, other) for d in range(NY)]
    for peer in peers:
        pl.semaphore_signal(barrier, inc=1, device_id=peer, device_id_type=MESH)

    xyz = xyz_ref[...]
    disp = disp_ref[...]
    zeros5 = jnp.zeros((5, OWN), f32)
    table = jnp.concatenate([disp, xyz, zeros5], axis=0)
    stacked = jnp.concatenate(
        [table[:, q * 128 : (q + 1) * 128] for q in range(4)], axis=0
    )
    tab[wide_id] = stacked.T
    own_xyz[0:3, :] = xyz
    vol = vol_ref[...]
    for h in range(2):
        vols[z, x, 3 * h : 3 * h + 3, :] = vol[:, h * 128 : (h + 1) * 128]
    near = near_ref[...]
    near_rows[...] = (near // OWN) * 128 + (near & 127)
    to_smem = pltpu.make_async_copy(near_rows, near_smem, local_sem)

    pl.semaphore_wait(barrier, len(peers))
    to_smem.start()

    def send(src, dst, send_sem, recv_sem, peer):
        copy = pltpu.make_async_remote_copy(
            src_ref=src, dst_ref=dst, send_sem=send_sem, recv_sem=recv_sem,
            device_id=peer, device_id_type=MESH,
        )
        copy.start()

    half = lambda w, h: tab.at[w, pl.ds(h * 64, 64), :]

    def landed(ref, sem):
        pltpu.make_async_copy(ref, ref, sem).wait()

    def send_x(w, h, number):
        for d in (1, 3, 2):
            send(half(w, h), half(w, h), x_send.at[number, d], chunk_recv.at[w, h], x_peer(d))

    def send_y(w, h, number):
        for d in (1, 3, 2):
            send(half(w, h), half(w, h), y_send.at[number, d], chunk_recv.at[w, h], y_peer(d))

    for h in range(2):
        send(half(wide_id, h), half(wide_id, h), z_send.at[h],
             chunk_recv.at[wide_id, h], z_peer(4))
    member = core * NY + y
    for d in range(1, NX):
        send(vols.at[z, x], vols.at[z, x], vx_send.at[d], vx_recv.at[x], x_peer(d))
    for c in range(2):
        for d in range(NY):
            if c or d:
                send(own_xyz, set_xyz.at[member], sx_send.at[c, d], sx_recv.at[member],
                     device(x, ys[d], z, core if c == 0 else other))
    send_x(wide_id, 0, 0)
    send_y(wide_id, 1, 0)
    send_y(wide_id, 0, 1)
    send_x(wide_id, 1, 1)

    for d in range(1, NX):
        landed(vols.at[z, xs[d]], vx_recv.at[xs[d]])
    for d in (4, 3, 5, 2, 6, 1, 7):
        send(vols.at[z], vols.at[z], vz_send.at[d], vz_recv.at[z], z_peer(d))

    set_xyz[member] = own_xyz[...]
    for c in range(2):
        for d in range(NY):
            who = (core if c == 0 else other) * NY + ys[d]
            if c or d:
                landed(set_xyz.at[who], sx_recv.at[who])
            rows = feature_rows(set_xyz[who], True)
            at = pl.multiple_of(who * OWN, OWN)
            fs[pl.ds(at, OWN), :] = rows.T.astype(bf16)

    for d in (0, 1, 7, 6, 2, 5, 3, 4):
        if d:
            landed(vols.at[zs[d]], vz_recv.at[zs[d]])
        parts = [vols[zs[d], k] for k in range(NX)]
        at_z = jnp.concatenate(
            [p[3 * h : 3 * h + 3] for p in parts for h in range(2)], axis=1
        )
        at = pl.multiple_of(zs[d] * (NX * VOWN), NX * VOWN)
        fv[:, pl.ds(at, NX * VOWN)] = feature_rows(at_z, False).astype(bf16)

    def place(order):
        p = lax.div(order, 2)
        z_to = lax.rem(z + z_offset(p), NZ)
        pair = lax.rem(lax.div(x, 2) + 1 + order, 2)
        return z_to, pair * 2

    def weights(order):
        z_to, x_to = place(order)
        at = pl.multiple_of((z_to * NX + x_to) * VOWN, TILE)
        radius = jnp.dot(fs[...], fv[:, pl.ds(at, TILE)], preferred_element_type=f32)
        return (1.0 / (radius * radius)).astype(bf16)

    def relay_near():
        for n, d in enumerate((1, 3, 2)):
            w = wide_at(xs[d], z_high, y)
            landed(half(w, 0), chunk_recv.at[w, 0])
            send_y(w, 0, 4 + n)
            w = wide_at(x, z_high, ys[d])
            landed(half(w, 1), chunk_recv.at[w, 1])
            send_x(w, 1, 4 + n)

    def start_far():
        far_w = wide_at(x, far_h, y)
        for h in range(2):
            landed(half(far_w, h), chunk_recv.at[far_w, h])
        send_x(far_w, 0, 2)
        send_y(far_w, 1, 2)
        send_y(far_w, 0, 3)
        send_x(far_w, 1, 3)

    def relay_far():
        for n, d in enumerate((1, 3, 2)):
            w = wide_at(xs[d], far_h, y)
            landed(half(w, 0), chunk_recv.at[w, 0])
            send_y(w, 0, 7 + n)
            w = wide_at(x, far_h, ys[d])
            landed(half(w, 1), chunk_recv.at[w, 1])
            send_x(w, 1, 7 + n)

    steps = dict(zip(RELAY_AT, (relay_near, start_far, relay_far)))

    def early(i, _):
        for at, step in steps.items():
            pl.when(i == at)(step)
        cache[CACHED - 1 - i] = weights(CACHED - 1 - i)
        return 0

    lax.fori_loop(0, EARLY, early, 0)

    for high in (z_high, far_h):
        for d in range(1, NX):
            for e in range(1, NY):
                w = wide_at(xs[d], high, ys[e])
                for h in range(2):
                    landed(half(w, h), chunk_recv.at[w, h])
        for d in range(1, NX):
            w = wide_at(xs[d], high, y)
            landed(half(w, 1), chunk_recv.at[w, 1])
            w = wide_at(x, high, ys[d])
            landed(half(w, 0), chunk_recv.at[w, 0])

    to_smem.wait()
    STEP = 8

    def pick(group, _):
        for k in range(STEP):
            j = group * STEP + k
            for n in range(4):
                row = near_smem[n, j]
                picked[n, pl.ds(j, 1), :] = tab[lax.div(row, 128), pl.ds(lax.rem(row, 128), 1), :]
        return 0

    lax.fori_loop(0, OWN // STEP, pick, 0)

    chosen = []
    for n in range(4):
        quarter = lax.rem(lax.div(near[n : n + 1], 128), 4)
        turned = picked[n].T
        value = turned[0:32]
        for q in range(1, 4):
            value = jnp.where(quarter == q, turned[q * 32 : (q + 1) * 32], value)
        chosen.append(value)
    first, second = chosen[0] - chosen[1], chosen[2] - chosen[3]

    def scaled(change):
        t = change[24:27]
        length = (t[0:1] * t[0:1] + t[1:2] * t[1:2]) + t[2:3] * t[2:3]
        return t / (length + tangent_floor)

    one, two = scaled(first), scaled(second)
    linear = [
        first[0:24] * one[q : q + 1] + second[0:24] * two[q : q + 1] for q in range(3)
    ]
    offset = (linear[0] * xyz[0:1] + linear[1] * xyz[1:2]) + linear[2] * xyz[2:3]
    tail = jnp.where(lax.broadcasted_iota(i32, (8, OWN), 0) == 0, 1.0, 0.0)
    own_blk[...] = jnp.concatenate(linear + [disp - offset, tail], axis=0).astype(bf16)

    def columns(who):
        return blk.at[:, pl.ds(pl.multiple_of(who * OWN, OWN), OWN)]

    own_copy = pltpu.make_async_copy(own_blk, columns(member), local_sem)
    own_copy.start()
    for d in (2, 1, 3):
        send(own_blk, columns(member), b_send.at[d], b_recv.at[member], y_peer(d))
    send(own_blk, columns(member), b_send.at[0], b_recv.at[member],
         device(x, y, z, other))
    own_copy.wait()

    def relay_blocks():
        for d in (1, 3, 2):
            who = core * NY + ys[d]
            landed(columns(who), b_recv.at[who])
            send(columns(who), columns(who), b_send.at[3 + d], b_recv.at[who],
                 device(x, y, z, other))

    def late(i, _):
        cache[CACHED - 1 - i] = weights(CACHED - 1 - i)
        pl.when(i == BLOCKS_AT)(relay_blocks)
        return 0

    lax.fori_loop(EARLY, CACHED, late, 0)

    for d in range(NY):
        who = other * NY + ys[d]
        landed(columns(who), b_recv.at[who])

    def x_copy(p, d):
        z_to = lax.rem(z + z_offset(p), NZ)
        return pltpu.make_async_remote_copy(
            src_ref=part.at[z_to, xs[d]], dst_ref=got_x.at[z_to, x],
            send_sem=rx_send.at[z_to, d], recv_sem=rx_recv.at[z_to, x],
            device_id=x_peer(d), device_id_type=MESH,
        )

    def z_copy(p):
        z_to = lax.rem(z + z_offset(p), NZ)
        return pltpu.make_async_remote_copy(
            src_ref=mid.at[z_to], dst_ref=got_z.at[z],
            send_sem=rz_send.at[z_to], recv_sem=rz_recv.at[z],
            device_id=device(x, y, z_to, core), device_id_type=MESH,
        )

    def collect(p):
        z_to = lax.rem(z + z_offset(p), NZ)
        total = part[z_to, x]
        for d in range(1, NX):
            landed(got_x.at[z_to, xs[d]], rx_recv.at[z_to, xs[d]])
            total = total + got_x[z_to, xs[d]]
        mid[z_to] = total

    def traffic(order):
        p = lax.div(order, 2)

        @pl.when(lax.rem(order, 2) == 0)
        def _():
            @pl.when(p >= 1)
            def _():
                for d in (2, 1, 3):
                    x_copy(p - 1, d).start()

            @pl.when(p >= LAG + 1)
            def _():
                z_copy(p - LAG - 1).start()

            @pl.when(p >= LAG)
            def _():
                collect(p - LAG)

    def finish_tile(order, weight):
        total = jnp.dot(blk[...], weight, preferred_element_type=f32)
        z_to, x_to = place(order)
        for k in range(PER_TILE):
            block = total[:, k * VOWN : (k + 1) * VOWN]
            raw = vols[z_to, x_to + k]
            at = jnp.concatenate([raw[0:3], raw[3:6]], axis=1)
            moved = (
                (block[0:24] * at[0:1] + block[24:48] * at[1:2]) + block[48:72] * at[2:3]
            ) + block[72:96]
            part[z_to, x_to + k] = jnp.concatenate([moved, block[96:104]], axis=0)

    def cached_tile(order, _):
        traffic(order)
        finish_tile(order, cache[order])
        return 0

    def fresh_tile(order, _):
        traffic(order)
        finish_tile(order, weights(order))
        return 0

    lax.fori_loop(0, CACHED, cached_tile, 0)
    lax.fori_loop(CACHED, TILES, fresh_tile, 0)

    for d in (2, 1, 3):
        x_copy(NZ - 1, d).start()
    for p in range(NZ - LAG, NZ):
        if p - 1 >= 0:
            z_copy(p - 1).start()
        collect(p)
    total = mid[z]
    for d in range(1, NZ):
        landed(got_z.at[zs[d]], rz_recv.at[zs[d]])
        total = total + got_z[zs[d]]
    out_ref[...] = total[0:24] / total[24:25]

    for h in range(2):
        landed(half(0, 0), z_send.at[h])
    for d in range(1, NX):
        landed(vols.at[0, 0], vx_send.at[d])
        for number in range(10):
            landed(half(0, 0), x_send.at[number, d])
            landed(half(0, 0), y_send.at[number, d])
    for d in range(1, NZ):
        landed(vols.at[0], vz_send.at[d])
    for c in range(2):
        for d in range(NY):
            if c or d:
                landed(own_xyz, sx_send.at[c, d])
    for number in range(7):
        landed(own_blk, b_send.at[number])
    for p in range(NZ):
        for d in range(1, NX):
            x_copy(p, d).wait_send()
        if p < NZ - 1:
            z_copy(p).wait_send()


def on_device(surf_xyz, surf_disp, neighbours, vol_xyz):
    dma = pltpu.SemaphoreType.DMA
    vmem = pl.BlockSpec(memory_space=pltpu.VMEM)
    return pl.pallas_call(
        kernel,
        out_shape=jax.ShapeDtypeStruct((24, VOWN), f32),
        in_specs=[vmem] * 4,
        out_specs=vmem,
        scratch_shapes=[
            pltpu.VMEM((32, 128, 128), f32),
            pltpu.VMEM((8, OWN), f32),
            pltpu.VMEM((SET, 8, OWN), f32),
            pltpu.VMEM((NZ, NX, 8, 128), f32),
            pltpu.VMEM((S_ALL, FEAT), bf16),
            pltpu.VMEM((FEAT, V_ALL), bf16),
            pltpu.VMEM((4, OWN, 128), f32),
            pltpu.VMEM((4, OWN), i32),
            pltpu.SMEM((4, OWN), i32),
            pltpu.VMEM((ROWS, OWN), bf16),
            pltpu.VMEM((ROWS, S_ALL), bf16),
            pltpu.VMEM((NZ, NX, 32, VOWN), f32),
            pltpu.VMEM((NZ, NX, 32, VOWN), f32),
            pltpu.VMEM((NZ, 32, VOWN), f32),
            pltpu.VMEM((NZ, 32, VOWN), f32),
            pltpu.VMEM((CACHED, S_ALL, TILE), bf16),
            dma((2,)), dma((10, NX)), dma((10, NY)), dma((32, 2)),
            dma((2, NY)), dma((SET,)), dma((NX,)), dma((NX,)),
            dma((NZ,)), dma((NZ,)), dma((8,)), dma((SET,)),
            dma((NZ, NX)), dma((NZ, NX)), dma((NZ,)), dma((NZ,)), dma,
        ],
        compiler_params=pltpu.CompilerParams(
            collective_id=0, has_side_effects=True, vmem_limit_bytes=67043328
        ),
        name="warp",
    )(surf_xyz, surf_disp, neighbours, vol_xyz)


def solution(mesh):
    spec = P(None, ("blk", "wide"))
    return jax.shard_map(
        on_device, mesh=mesh, in_specs=(spec,) * 4, out_specs=spec, check_vma=False
    )
```

```python
import jax
import jax.numpy as jnp
from jax import lax
from jax.experimental import pallas as pl
from jax.experimental.pallas import tpu as pltpu
from jax.sharding import PartitionSpec as P

MESH = pl.DeviceIdType.MESH
tangent_floor = 0.04
core_radius = 0.04
f32, bf16, i32 = jnp.float32, jnp.bfloat16, jnp.int32

NX, NY, NZ = 4, 4, 8
LOW = 4
OWN = 512
VOWN = 256
TILE = 512
SET = 8
S_ALL = SET * OWN
V_SLOTS = NX * NZ
V_ALL = V_SLOTS * VOWN
PER_TILE = TILE // VOWN
TILES = V_ALL // TILE
ROWS = 104
FEAT = 32
CACHED = 9
EARLY = 5
RELAY_AT = 1
BLOCKS_AT = 7
LAG = 3


def device(x, y, z, core):
    return (lax.rem(z, LOW) * 2 + core, (x * 2 + lax.div(z, LOW)) * NY + y)


def z_offset(p):
    if isinstance(p, int):
        return 4 + (1 - 2 * (p % 2)) * ((p + 1) // 2)
    return 4 + (1 - 2 * lax.rem(p, 2)) * lax.div(p + 1, 2)


def split(value):
    high = value.astype(bf16).astype(f32)
    rest = value - high
    middle = rest.astype(bf16).astype(f32)
    return high, middle, (rest - middle).astype(bf16).astype(f32)


PAIRS = ((0, 0), (0, 1), (1, 0), (0, 2), (2, 0), (1, 1), (1, 2), (2, 1))


def feature_rows(xyz, surface):
    count = xyz.shape[1]
    ones = jnp.ones((1, count), f32)
    rows = []
    scale = 1.0 if surface else -2.0
    norm = (xyz[0:1] * xyz[0:1] + xyz[1:2] * xyz[1:2]) + xyz[2:3] * xyz[2:3]
    for axis in range(3):
        parts = split(xyz[axis : axis + 1] * scale)
        rows += [parts[pair[0] if surface else pair[1]] for pair in PAIRS]
    if surface:
        rows += list(split(norm + core_radius)) + [ones] * 3
    else:
        rows += [ones] * 3 + list(split(norm))
    rows += [jnp.zeros((1, count), f32)] * (FEAT - len(rows))
    return jnp.concatenate(rows, axis=0)


def kernel(
    xyz_ref, disp_ref, near_ref, vol_ref, out_ref,
    tab, own_xyz, set_xyz, vols, fs, fv, picked, near_rows, near_smem,
    own_blk, blk, part, got_x, mid, got_z, cache,
    chunk_send, near_recv, far_recv, twin_recv, rest_recv, sx_send, sx_recv,
    vx_send, vx_recv, vz_send, vz_recv, b_send, b_recv, sibling_recv,
    rx_send, rx_recv, rz_send, rz_recv, local_sem,
):
    blk_id, wide_id = lax.axis_index("blk"), lax.axis_index("wide")
    core = lax.rem(blk_id, 2)
    z_low = lax.div(blk_id, 2)
    y = lax.rem(wide_id, NY)
    z_high = lax.rem(lax.div(wide_id, NY), 2)
    x = lax.div(wide_id, NY * 2)
    z = z_high * LOW + z_low
    other = 1 - core
    wide_at = lambda ax, ah, ay: (ax * 2 + ah) * NY + ay
    xs = [lax.rem(x + d, NX) for d in range(NX)]
    ys = [lax.rem(y + d, NY) for d in range(NY)]
    zs = [lax.rem(z + d, NZ) for d in range(NZ)]
    far_h = 1 - z_high
    x_peer = lambda d: device(xs[d], y, z, core)
    y_peer = lambda d: device(x, ys[d], z, core)
    z_peer = lambda d: device(x, y, zs[d], core)

    barrier = pltpu.get_barrier_semaphore()
    peers = [z_peer(4)] + [x_peer(d) for d in range(1, NX)]
    peers += [y_peer(d) for d in range(1, NY)]
    peers += [z_peer(d) for d in (3, 5, 2, 6, 1, 7)]
    peers += [device(x, ys[d], z, other) for d in range(NY)]
    for peer in peers:
        pl.semaphore_signal(barrier, inc=1, device_id=peer, device_id_type=MESH)

    xyz = xyz_ref[...]
    disp = disp_ref[...]
    zeros5 = jnp.zeros((5, OWN), f32)
    table = jnp.concatenate([disp, xyz, zeros5], axis=0)
    stacked = jnp.concatenate(
        [table[:, q * 128 : (q + 1) * 128] for q in range(4)], axis=0
    )
    tab[pl.ds(pl.multiple_of(wide_id * 128, 128), 128), :] = stacked.T
    own_xyz[0:3, :] = xyz
    vol = vol_ref[...]
    for h in range(2):
        vols[z, x, 3 * h : 3 * h + 3, :] = vol[:, h * 128 : (h + 1) * 128]
    near = near_ref[...]
    near_rows[...] = (near // OWN) * 128 + (near & 127)
    to_smem = pltpu.make_async_copy(near_rows, near_smem, local_sem.at[0])

    pl.semaphore_wait(barrier, len(peers))
    to_smem.start()

    def send(src, dst, send_sem, recv_sem, peer):
        copy = pltpu.make_async_remote_copy(
            src_ref=src, dst_ref=dst, send_sem=send_sem, recv_sem=recv_sem,
            device_id=peer, device_id_type=MESH,
        )
        copy.start()

    half = lambda w, h: tab.at[pl.ds(pl.multiple_of(w * 128 + h * 64, 64), 64), :]

    def landed(ref, sem):
        pltpu.make_async_copy(ref, ref, sem).wait()

    def send_x(w, h, recv=None):
        for d in (1, 3, 2):
            sem = rest_recv if recv is None else recv.at[0, NX - d]
            send(half(w, h), half(w, h), chunk_send, sem, x_peer(d))

    def send_y(w, h, recv=None):
        for d in (1, 3, 2):
            sem = rest_recv if recv is None else recv.at[1, NY - d]
            send(half(w, h), half(w, h), chunk_send, sem, y_peer(d))

    for h in range(2):
        send(half(wide_id, h), half(wide_id, h), chunk_send, twin_recv, z_peer(4))
    member = core * NY + y
    for d in range(1, NX):
        send(vols.at[z, x], vols.at[z, x], vx_send, vx_recv, x_peer(d))
    send_x(wide_id, 0, near_recv)
    send_y(wide_id, 1, near_recv)
    for c in range(2):
        for d in range(NY):
            if c or d:
                send(own_xyz, set_xyz.at[member], sx_send, sx_recv,
                     device(x, ys[d], z, core if c == 0 else other))
    send_y(wide_id, 0)
    send_x(wide_id, 1)
    set_xyz[member] = own_xyz[...]

    landed(vols.at[0, pl.ds(0, NX - 1)], vx_recv)
    for d in (4, 3, 5, 2, 6, 1, 7):
        send(vols.at[z], vols.at[z], vz_send, vz_recv, z_peer(d))

    def relay_near():
        for d in (1, 3, 2):
            w = wide_at(xs[d], z_high, y)
            landed(half(w, 0), near_recv.at[0, d])
            send_y(w, 0)
            w = wide_at(x, z_high, ys[d])
            landed(half(w, 1), near_recv.at[1, d])
            send_x(w, 1)

    def start_far():
        far_w = wide_at(x, far_h, y)
        landed(tab.at[pl.ds(pl.multiple_of(far_w * 128, 128), 128), :], twin_recv)
        send_x(far_w, 0, far_recv)
        send_y(far_w, 1, far_recv)
        send_y(far_w, 0)
        send_x(far_w, 1)

    def relay_far():
        for d in (1, 3, 2):
            w = wide_at(xs[d], far_h, y)
            landed(half(w, 0), far_recv.at[0, d])
            send_y(w, 0)
            w = wide_at(x, far_h, ys[d])
            landed(half(w, 1), far_recv.at[1, d])
            send_x(w, 1)

    relay_near()

    landed(set_xyz.at[pl.ds(0, SET - 1)], sx_recv)
    for who in range(SET):
        rows = feature_rows(set_xyz[who], True)
        fs[who * OWN : (who + 1) * OWN, :] = rows.T.astype(bf16)

    start_far()

    landed(vols.at[pl.ds(0, NZ - 1)], vz_recv)
    for k in range(NZ):
        parts = [vols[k, j] for j in range(NX)]
        at_z = jnp.concatenate(
            [p[3 * h : 3 * h + 3] for p in parts for h in range(2)], axis=1
        )
        width = NX * VOWN
        fv[:, k * width : (k + 1) * width] = feature_rows(at_z, False).astype(bf16)

    def place(order):
        p = lax.div(order, 2)
        z_to = lax.rem(z + z_offset(p), NZ)
        pair = lax.rem(lax.div(x, 2) + 1 + order, 2)
        return z_to, pair * 2

    def weights(order):
        z_to, x_to = place(order)
        at = pl.multiple_of((z_to * NX + x_to) * VOWN, TILE)
        radius = jnp.dot(fs[...], fv[:, pl.ds(at, TILE)], preferred_element_type=f32)
        return (1.0 / (radius * radius)).astype(bf16)

    def early(i, _):
        pl.when(i == RELAY_AT)(relay_far)
        cache[CACHED - 1 - i] = weights(CACHED - 1 - i)
        return 0

    lax.fori_loop(0, EARLY, early, 0)

    landed(tab.at[pl.ds(0, 24 * 128), :], rest_recv)

    to_smem.wait()
    STEP = 16
    PART = OWN // 2

    def pick(group, _):
        for k in range(STEP):
            j = group * STEP + k
            for n in range(4):
                picked[n, pl.ds(j, 1), :] = tab[pl.ds(near_smem[n, j], 1), :]
        return 0

    def scaled(change):
        t = change[24:27]
        length = (t[0:1] * t[0:1] + t[1:2] * t[1:2]) + t[2:3] * t[2:3]
        return t / (length + tangent_floor)

    def columns(who, h=None):
        at = who * OWN + (h or 0) * PART
        size = OWN if h is None else PART
        return blk.at[:, pl.ds(pl.multiple_of(at, PART), size)]

    def build(h):
        at = slice(h * PART, (h + 1) * PART)
        chosen = []
        for n in range(4):
            quarter = lax.rem(lax.div(near[n : n + 1, at], 128), 4)
            turned = picked[n, at].T
            value = turned[0:32]
            for q in range(1, 4):
                value = jnp.where(quarter == q, turned[q * 32 : (q + 1) * 32], value)
            chosen.append(value)
        first, second = chosen[0] - chosen[1], chosen[2] - chosen[3]
        one, two = scaled(first), scaled(second)
        linear = [
            first[0:24] * one[q : q + 1] + second[0:24] * two[q : q + 1]
            for q in range(3)
        ]
        place_y = xyz[:, at]
        offset = (
            linear[0] * place_y[0:1] + linear[1] * place_y[1:2]
        ) + linear[2] * place_y[2:3]
        tail = jnp.where(lax.broadcasted_iota(i32, (8, PART), 0) == 0, 1.0, 0.0)
        own_blk[h] = jnp.concatenate(
            linear + [disp[:, at] - offset, tail], axis=0
        ).astype(bf16)

    own_copies = []
    for h in range(2):
        lax.fori_loop(h * PART // STEP, (h + 1) * PART // STEP, pick, 0)
        build(h)
        for d in (2, 1, 3):
            send(own_blk.at[h], columns(member, h), b_send, b_recv.at[NY - d], y_peer(d))
        send(own_blk.at[h], columns(member, h), b_send, sibling_recv,
             device(x, y, z, other))
        copy = pltpu.make_async_copy(own_blk.at[h], columns(member, h), local_sem.at[h])
        copy.start()
        own_copies.append(copy)

    for copy in own_copies:
        copy.wait()

    def relay_blocks():
        for d in (1, 3, 2):
            who = core * NY + ys[d]
            landed(columns(who), b_recv.at[d])
            send(columns(who), columns(who), b_send, sibling_recv,
                 device(x, y, z, other))

    def late(i, _):
        cache[CACHED - 1 - i] = weights(CACHED - 1 - i)
        pl.when(i == BLOCKS_AT)(relay_blocks)
        return 0

    lax.fori_loop(EARLY, CACHED, late, 0)

    landed(blk.at[:, pl.ds(0, NY * OWN)], sibling_recv)

    def x_copy(p, d):
        z_to = lax.rem(z + z_offset(p), NZ)
        return pltpu.make_async_remote_copy(
            src_ref=part.at[z_to, xs[d]], dst_ref=got_x.at[z_to, x],
            send_sem=rx_send, recv_sem=rx_recv.at[z_to],
            device_id=x_peer(d), device_id_type=MESH,
        )

    def z_copy(p):
        z_to = lax.rem(z + z_offset(p), NZ)
        return pltpu.make_async_remote_copy(
            src_ref=mid.at[z_to], dst_ref=got_z.at[z],
            send_sem=rz_send, recv_sem=rz_recv,
            device_id=device(x, y, z_to, core), device_id_type=MESH,
        )

    def collect(p):
        z_to = lax.rem(z + z_offset(p), NZ)
        total = part[z_to, x]
        landed(got_x.at[z_to, pl.ds(0, NX - 1)], rx_recv.at[z_to])
        for d in range(1, NX):
            total = total + got_x[z_to, xs[d]]
        mid[z_to] = total

    def traffic(order):
        p = lax.div(order, 2)

        @pl.when(lax.rem(order, 2) == 0)
        def _():
            @pl.when(p >= 1)
            def _():
                for d in (2, 1, 3):
                    x_copy(p - 1, d).start()

            @pl.when(p >= LAG + 1)
            def _():
                z_copy(p - LAG - 1).start()

            @pl.when(p >= LAG)
            def _():
                collect(p - LAG)

    def finish_tile(order, weight):
        total = jnp.dot(blk[...], weight, preferred_element_type=f32)
        z_to, x_to = place(order)
        for k in range(PER_TILE):
            block = total[:, k * VOWN : (k + 1) * VOWN]
            raw = vols[z_to, x_to + k]
            at = jnp.concatenate([raw[0:3], raw[3:6]], axis=1)
            moved = (
                (block[0:24] * at[0:1] + block[24:48] * at[1:2]) + block[48:72] * at[2:3]
            ) + block[72:96]
            part[z_to, x_to + k] = jnp.concatenate([moved, block[96:104]], axis=0)

    def cached_tile(order, _):
        traffic(order)
        finish_tile(order, cache[order])
        return 0

    def fresh_tile(order, _):
        traffic(order)
        finish_tile(order, weights(order))
        return 0

    lax.fori_loop(0, CACHED, cached_tile, 0)
    lax.fori_loop(CACHED, TILES, fresh_tile, 0)

    for d in (2, 1, 3):
        x_copy(NZ - 1, d).start()
    for p in range(NZ - LAG, NZ):
        if p - 1 >= 0:
            z_copy(p - 1).start()
        collect(p)
    total = mid[z]
    landed(got_z.at[pl.ds(0, NZ - 1)], rz_recv)
    for d in range(1, NZ):
        total = total + got_z[zs[d]]
    out_ref[...] = total[0:24] / total[24:25]

    landed(tab.at[pl.ds(0, 31 * 128), :], chunk_send)
    landed(vols.at[0, pl.ds(0, NX - 1)], vx_send)
    landed(vols.at[pl.ds(0, NZ - 1)], vz_send)
    landed(set_xyz.at[pl.ds(0, SET - 1)], sx_send)
    landed(blk.at[:, pl.ds(0, 7 * OWN)], b_send)
    landed(part.at[:, pl.ds(0, NX - 1)], rx_send)
    landed(mid.at[pl.ds(0, NZ - 1)], rz_send)


def on_device(surf_xyz, surf_disp, neighbours, vol_xyz):
    dma = pltpu.SemaphoreType.DMA
    vmem = pl.BlockSpec(memory_space=pltpu.VMEM)
    return pl.pallas_call(
        kernel,
        out_shape=jax.ShapeDtypeStruct((24, VOWN), f32),
        in_specs=[vmem] * 4,
        out_specs=vmem,
        scratch_shapes=[
            pltpu.VMEM((32 * 128, 128), f32),
            pltpu.VMEM((8, OWN), f32),
            pltpu.VMEM((SET, 8, OWN), f32),
            pltpu.VMEM((NZ, NX, 8, 128), f32),
            pltpu.VMEM((S_ALL, FEAT), bf16),
            pltpu.VMEM((FEAT, V_ALL), bf16),
            pltpu.VMEM((4, OWN, 128), f32),
            pltpu.VMEM((4, OWN), i32),
            pltpu.SMEM((4, OWN), i32),
            pltpu.VMEM((2, ROWS, OWN // 2), bf16),
            pltpu.VMEM((ROWS, S_ALL), bf16),
            pltpu.VMEM((NZ, NX, 32, VOWN), f32),
            pltpu.VMEM((NZ, NX, 32, VOWN), f32),
            pltpu.VMEM((NZ, 32, VOWN), f32),
            pltpu.VMEM((NZ, 32, VOWN), f32),
            pltpu.VMEM((CACHED, S_ALL, TILE), bf16),
            dma, dma((2, NX)), dma((2, NX)), dma, dma, dma, dma,
            dma, dma, dma, dma, dma, dma((NY,)), dma,
            dma, dma((NZ,)), dma, dma, dma((2,)),
        ],
        compiler_params=pltpu.CompilerParams(
            collective_id=0, has_side_effects=True, vmem_limit_bytes=67043328
        ),
        name="warp",
    )(surf_xyz, surf_disp, neighbours, vol_xyz)


def solution(mesh):
    spec = P(None, ("blk", "wide"))
    return jax.shard_map(
        on_device, mesh=mesh, in_specs=(spec,) * 4, out_specs=spec, check_vma=False
    )
```

```python
import jax
import jax.numpy as jnp
from jax import lax
from jax.experimental import pallas as pl
from jax.experimental.pallas import tpu as pltpu
from jax.sharding import PartitionSpec as P

MESH = pl.DeviceIdType.MESH
tangent_floor = 0.04
core_radius = 0.04
f32, bf16, i32 = jnp.float32, jnp.bfloat16, jnp.int32

NX, NY, NZ = 4, 4, 8
LOW = 4
OWN = 512
VOWN = 256
TILE = 512
SET = 8
S_ALL = SET * OWN
V_SLOTS = NX * NZ
V_ALL = V_SLOTS * VOWN
PER_TILE = TILE // VOWN
TILES = V_ALL // TILE
ROWS = 104
FEAT = 32
CACHED = 9
EARLY = 5
RELAY_AT = 1
BLOCKS_AT = 7
CHUNK = 4096


def device(x, y, z, core):
    return (lax.rem(z, LOW) * 2 + core, (x * 2 + lax.div(z, LOW)) * NY + y)


def z_offset(p):
    if isinstance(p, int):
        return 4 + (1 - 2 * (p % 2)) * ((p + 1) // 2)
    return 4 + (1 - 2 * lax.rem(p, 2)) * lax.div(p + 1, 2)


def split(value):
    high = value.astype(bf16).astype(f32)
    rest = value - high
    middle = rest.astype(bf16).astype(f32)
    return high, middle, (rest - middle).astype(bf16).astype(f32)


PAIRS = ((0, 0), (0, 1), (1, 0), (0, 2), (2, 0), (1, 1), (1, 2), (2, 1))


def feature_rows(xyz, surface):
    count = xyz.shape[1]
    ones = jnp.ones((1, count), f32)
    rows = []
    scale = 1.0 if surface else -2.0
    norm = (xyz[0:1] * xyz[0:1] + xyz[1:2] * xyz[1:2]) + xyz[2:3] * xyz[2:3]
    for axis in range(3):
        parts = split(xyz[axis : axis + 1] * scale)
        rows += [parts[pair[0] if surface else pair[1]] for pair in PAIRS]
    if surface:
        rows += list(split(norm + core_radius)) + [ones] * 3
    else:
        rows += [ones] * 3 + list(split(norm))
    rows += [jnp.zeros((1, count), f32)] * (FEAT - len(rows))
    return jnp.concatenate(rows, axis=0)


def kernel(
    xyz_ref, disp_ref, near_ref, vol_ref, out_ref,
    tab, own_xyz, set_xyz, vols, fs, fv, picked, near_rows, near_smem,
    own_blk, blk, part, got_x, mid, got_z, cache,
    chunk_send, near_recv, far_recv, twin_recv, rest_recv, sx_send, sx_recv,
    vx_send, vx_recv, vz_send, vz_recv, b_send, b_recv, sibling_recv,
    rx_send, rx_recv, rz_send, rz_recv, local_sem,
):
    blk_id, wide_id = lax.axis_index("blk"), lax.axis_index("wide")
    core = lax.rem(blk_id, 2)
    z_low = lax.div(blk_id, 2)
    y = lax.rem(wide_id, NY)
    z_high = lax.rem(lax.div(wide_id, NY), 2)
    x = lax.div(wide_id, NY * 2)
    z = z_high * LOW + z_low
    other = 1 - core
    wide_at = lambda ax, ah, ay: (ax * 2 + ah) * NY + ay
    xs = [lax.rem(x + d, NX) for d in range(NX)]
    ys = [lax.rem(y + d, NY) for d in range(NY)]
    zs = [lax.rem(z + d, NZ) for d in range(NZ)]
    far_h = 1 - z_high
    x_peer = lambda d: device(xs[d], y, z, core)
    y_peer = lambda d: device(x, ys[d], z, core)
    z_peer = lambda d: device(x, y, zs[d], core)

    barrier = pltpu.get_barrier_semaphore()
    peers = [z_peer(4)] + [x_peer(d) for d in range(1, NX)]
    peers += [y_peer(d) for d in range(1, NY)]
    peers += [z_peer(d) for d in (3, 5, 2, 6, 1, 7)]
    peers += [device(x, ys[d], z, other) for d in range(NY)]
    for peer in peers:
        pl.semaphore_signal(barrier, inc=1, device_id=peer, device_id_type=MESH)

    xyz = xyz_ref[...]
    disp = disp_ref[...]
    zeros5 = jnp.zeros((5, OWN), f32)
    table = jnp.concatenate([disp, xyz, zeros5], axis=0)
    stacked = jnp.concatenate(
        [table[:, q * 128 : (q + 1) * 128] for q in range(4)], axis=0
    )
    tab[pl.ds(pl.multiple_of(wide_id * 128, 128), 128), :] = stacked.T
    own_xyz[0:3, :] = xyz
    vol = vol_ref[...]
    for h in range(2):
        vols[z, x, 3 * h : 3 * h + 3, :] = vol[:, h * 128 : (h + 1) * 128]
    near = near_ref[...]
    rows = (near // OWN) * 128 + (near & 127)
    lines = [rows[:, b * 128 : (b + 1) * 128] for b in range(4)]
    near_rows[...] = jnp.concatenate(lines + [jnp.zeros((112, 128), i32)], axis=0).T
    to_smem = pltpu.make_async_copy(near_rows, near_smem, local_sem.at[0])

    pl.semaphore_wait(barrier, len(peers))
    to_smem.start()

    def send(src, dst, send_sem, recv_sem, peer):
        copy = pltpu.make_async_remote_copy(
            src_ref=src, dst_ref=dst, send_sem=send_sem, recv_sem=recv_sem,
            device_id=peer, device_id_type=MESH,
        )
        copy.start()

    half = lambda w, h: tab.at[pl.ds(pl.multiple_of(w * 128 + h * 64, 64), 64), :]

    def landed(ref, sem):
        pltpu.make_async_copy(ref, ref, sem).wait()

    def send_x(w, h, recv=None):
        for d in (1, 3, 2):
            sem = rest_recv if recv is None else recv.at[0, NX - d]
            send(half(w, h), half(w, h), chunk_send, sem, x_peer(d))

    def send_y(w, h, recv=None):
        for d in (1, 3, 2):
            sem = rest_recv if recv is None else recv.at[1, NY - d]
            send(half(w, h), half(w, h), chunk_send, sem, y_peer(d))

    for h in range(2):
        send(half(wide_id, h), half(wide_id, h), chunk_send, twin_recv, z_peer(4))
    member = core * NY + y
    for d in range(1, NX):
        send(vols.at[z, x], vols.at[z, x], vx_send, vx_recv, x_peer(d))
    for c in range(2):
        for d in range(NY):
            if c or d:
                send(own_xyz, set_xyz.at[member], sx_send, sx_recv,
                     device(x, ys[d], z, core if c == 0 else other))
    send_x(wide_id, 0, near_recv)
    send_y(wide_id, 1, near_recv)
    send_y(wide_id, 0)
    send_x(wide_id, 1)
    set_xyz[member] = own_xyz[...]

    landed(vols.at[0, pl.ds(0, NX - 1)], vx_recv)
    for d in (4, 3, 5, 2, 6, 1, 7):
        send(vols.at[z], vols.at[z], vz_send, vz_recv, z_peer(d))

    def relay_near():
        for d in (1, 3, 2):
            w = wide_at(xs[d], z_high, y)
            landed(half(w, 0), near_recv.at[0, d])
            send_y(w, 0)
            w = wide_at(x, z_high, ys[d])
            landed(half(w, 1), near_recv.at[1, d])
            send_x(w, 1)

    def start_far():
        far_w = wide_at(x, far_h, y)
        landed(tab.at[pl.ds(pl.multiple_of(far_w * 128, 128), 128), :], twin_recv)
        send_x(far_w, 0, far_recv)
        send_y(far_w, 1, far_recv)
        send_y(far_w, 0)
        send_x(far_w, 1)

    def relay_far():
        for d in (1, 3, 2):
            w = wide_at(xs[d], far_h, y)
            landed(half(w, 0), far_recv.at[0, d])
            send_y(w, 0)
            w = wide_at(x, far_h, ys[d])
            landed(half(w, 1), far_recv.at[1, d])
            send_x(w, 1)

    relay_near()

    landed(set_xyz.at[pl.ds(0, SET - 1)], sx_recv)
    for who in range(SET):
        rows = feature_rows(set_xyz[who], True)
        fs[who * OWN : (who + 1) * OWN, :] = rows.T.astype(bf16)

    start_far()

    landed(vols.at[pl.ds(0, NZ - 1)], vz_recv)
    for k in range(NZ):
        parts = [vols[k, j] for j in range(NX)]
        at_z = jnp.concatenate(
            [p[3 * h : 3 * h + 3] for p in parts for h in range(2)], axis=1
        )
        width = NX * VOWN
        fv[:, k * width : (k + 1) * width] = feature_rows(at_z, False).astype(bf16)

    def place(order):
        p = lax.div(order, 2)
        z_to = lax.rem(z + z_offset(p), NZ)
        pair = lax.rem(lax.div(x, 2) + 1 + order, 2)
        return z_to, pair * 2

    def weights(order, start=0, size=S_ALL):
        z_to, x_to = place(order)
        at = pl.multiple_of((z_to * NX + x_to) * VOWN, TILE)
        radius = jnp.dot(
            fs[start : start + size, :], fv[:, pl.ds(at, TILE)], preferred_element_type=f32
        )
        return (1.0 / (radius * radius)).astype(bf16)

    def early(i, _):
        pl.when(i == RELAY_AT)(relay_far)
        cache[CACHED - 1 - i] = weights(CACHED - 1 - i)
        return 0

    lax.fori_loop(0, EARLY, early, 0)

    landed(tab.at[pl.ds(0, 24 * 128), :], rest_recv)

    to_smem.wait()
    STEP = 8
    PART = OWN // 2

    def pick(h, group):
        for k in range(STEP):
            c = group * STEP + k
            for b in (2 * h, 2 * h + 1):
                for n in range(4):
                    picked[n, pl.ds(b * 128 + c, 1), :] = tab[
                        pl.ds(near_smem[c, 4 * b + n], 1), :
                    ]

    def scaled(change):
        t = change[24:27]
        length = (t[0:1] * t[0:1] + t[1:2] * t[1:2]) + t[2:3] * t[2:3]
        return t / (length + tangent_floor)

    def columns(who, h=None):
        at = who * OWN + (h or 0) * PART
        size = OWN if h is None else PART
        return blk.at[:, pl.ds(pl.multiple_of(at, PART), size)]

    def build(h):
        at = slice(h * PART, (h + 1) * PART)
        chosen = []
        for n in range(4):
            quarter = lax.rem(lax.div(near[n : n + 1, at], 128), 4)
            turned = picked[n, at].T
            value = turned[0:32]
            for q in range(1, 4):
                value = jnp.where(quarter == q, turned[q * 32 : (q + 1) * 32], value)
            chosen.append(value)
        first, second = chosen[0] - chosen[1], chosen[2] - chosen[3]
        one, two = scaled(first), scaled(second)
        linear = [
            first[0:24] * one[q : q + 1] + second[0:24] * two[q : q + 1]
            for q in range(3)
        ]
        place_y = xyz[:, at]
        offset = (
            linear[0] * place_y[0:1] + linear[1] * place_y[1:2]
        ) + linear[2] * place_y[2:3]
        tail = jnp.where(lax.broadcasted_iota(i32, (8, PART), 0) == 0, 1.0, 0.0)
        own_blk[h] = jnp.concatenate(
            linear + [disp[:, at] - offset, tail], axis=0
        ).astype(bf16)

    own_copies = []
    for h in range(2):

        def half_pick(group, _, h=h):
            pick(h, group)
            return 0

        lax.fori_loop(0, 128 // STEP, half_pick, 0)
        build(h)
        for d in (2, 1, 3):
            send(own_blk.at[h], columns(member, h), b_send, b_recv.at[NY - d], y_peer(d))
        send(own_blk.at[h], columns(member, h), b_send, sibling_recv,
             device(x, y, z, other))
        copy = pltpu.make_async_copy(own_blk.at[h], columns(member, h), local_sem.at[h])
        copy.start()
        own_copies.append(copy)

    for copy in own_copies:
        copy.wait()

    def relay_blocks():
        for d in (1, 3, 2):
            who = core * NY + ys[d]
            landed(columns(who), b_recv.at[d])
            send(columns(who), columns(who), b_send, sibling_recv,
                 device(x, y, z, other))

    def late(i, _):
        cache[CACHED - 1 - i] = weights(CACHED - 1 - i)
        pl.when(i == BLOCKS_AT)(relay_blocks)
        return 0

    lax.fori_loop(EARLY, CACHED, late, 0)

    landed(blk.at[:, pl.ds(0, NY * OWN)], sibling_recv)

    def x_copy(z_to, x_to):
        return pltpu.make_async_remote_copy(
            src_ref=part.at[z_to, x_to], dst_ref=got_x.at[z_to, x],
            send_sem=rx_send, recv_sem=rx_recv.at[z_to],
            device_id=device(x_to, y, z, core), device_id_type=MESH,
        )

    def pass_x(order):
        z_to, x_to = place(order)

        @pl.when(lax.rem(order, 2) == 0)
        def _():
            for k in range(PER_TILE):
                x_copy(z_to, x_to + k).start()

        @pl.when(lax.rem(order, 2) == 1)
        def _():
            x_copy(z_to, x_to + 1 - lax.rem(x, 2)).start()

    def z_copy(p):
        z_to = lax.rem(z + z_offset(p), NZ)
        return pltpu.make_async_remote_copy(
            src_ref=mid.at[z_to], dst_ref=got_z.at[z],
            send_sem=rz_send, recv_sem=rz_recv,
            device_id=device(x, y, z_to, core), device_id_type=MESH,
        ).start()

    def collect(p):
        z_to = lax.rem(z + z_offset(p), NZ)
        total = part[z_to, x]
        landed(got_x.at[z_to, pl.ds(0, NX - 1)], rx_recv.at[z_to])
        for d in range(1, NX):
            total = total + got_x[z_to, xs[d]]
        mid[z_to] = total

    def traffic(order):
        even = lax.rem(order, 2) == 0
        odd = lax.rem(order, 2) == 1

        @pl.when(order >= 1)
        def _():
            pass_x(order - 1)

        @pl.when(odd & (order >= 7) & (order <= 11))
        def _():
            z_copy(lax.div(order - 7, 2))

        @pl.when(even & (order >= 12))
        def _():
            z_copy(lax.div(order - 6, 2))

        @pl.when(even & (order >= 6) & (order <= 10))
        def _():
            collect(lax.div(order - 6, 2))

        @pl.when(odd & (order >= 11))
        def _():
            collect(lax.div(order - 5, 2))

    def finish_tile(order, total):
        z_to, x_to = place(order)
        for k in range(PER_TILE):
            block = total[:, k * VOWN : (k + 1) * VOWN]
            raw = vols[z_to, x_to + k]
            at = jnp.concatenate([raw[0:3], raw[3:6]], axis=1)
            moved = (
                (block[0:24] * at[0:1] + block[24:48] * at[1:2]) + block[48:72] * at[2:3]
            ) + block[72:96]
            part[z_to, x_to + k] = jnp.concatenate([moved, block[96:104]], axis=0)

    def cached_tile(order, _):
        traffic(order)
        finish_tile(
            order, jnp.dot(blk[...], cache[order], preferred_element_type=f32)
        )
        return 0

    def fresh_tile(order, _):
        traffic(order)
        total = jnp.zeros((ROWS, TILE), f32)
        for at in range(0, S_ALL, CHUNK):
            total = total + jnp.dot(
                blk[:, at : at + CHUNK],
                weights(order, at, CHUNK),
                preferred_element_type=f32,
            )
        finish_tile(order, total)
        return 0

    lax.fori_loop(0, CACHED, cached_tile, 0)
    lax.fori_loop(CACHED, TILES, fresh_tile, 0)

    pass_x(TILES - 1)
    z_copy(5)
    collect(6)
    z_copy(6)
    collect(7)
    total = mid[z]
    landed(got_z.at[pl.ds(0, NZ - 1)], rz_recv)
    for d in range(1, NZ):
        total = total + got_z[zs[d]]
    out_ref[...] = total[0:24] / total[24:25]

    landed(tab.at[pl.ds(0, 31 * 128), :], chunk_send)
    landed(vols.at[0, pl.ds(0, NX - 1)], vx_send)
    landed(vols.at[pl.ds(0, NZ - 1)], vz_send)
    landed(set_xyz.at[pl.ds(0, SET - 1)], sx_send)
    landed(blk.at[:, pl.ds(0, 7 * OWN)], b_send)
    landed(part.at[:, pl.ds(0, NX - 1)], rx_send)
    landed(mid.at[pl.ds(0, NZ - 1)], rz_send)


def on_device(surf_xyz, surf_disp, neighbours, vol_xyz):
    dma = pltpu.SemaphoreType.DMA
    vmem = pl.BlockSpec(memory_space=pltpu.VMEM)
    return pl.pallas_call(
        kernel,
        out_shape=jax.ShapeDtypeStruct((24, VOWN), f32),
        in_specs=[vmem] * 4,
        out_specs=vmem,
        scratch_shapes=[
            pltpu.VMEM((32 * 128, 128), f32),
            pltpu.VMEM((8, OWN), f32),
            pltpu.VMEM((SET, 8, OWN), f32),
            pltpu.VMEM((NZ, NX, 8, 128), f32),
            pltpu.VMEM((S_ALL, FEAT), bf16),
            pltpu.VMEM((FEAT, V_ALL), bf16),
            pltpu.VMEM((4, OWN, 128), f32),
            pltpu.VMEM((128, 128), i32),
            pltpu.SMEM((128, 128), i32),
            pltpu.VMEM((2, ROWS, OWN // 2), bf16),
            pltpu.VMEM((ROWS, S_ALL), bf16),
            pltpu.VMEM((NZ, NX, 32, VOWN), f32),
            pltpu.VMEM((NZ, NX, 32, VOWN), f32),
            pltpu.VMEM((NZ, 32, VOWN), f32),
            pltpu.VMEM((NZ, 32, VOWN), f32),
            pltpu.VMEM((CACHED, S_ALL, TILE), bf16),
            dma, dma((2, NX)), dma((2, NX)), dma, dma, dma, dma,
            dma, dma, dma, dma, dma, dma((NY,)), dma,
            dma, dma((NZ,)), dma, dma, dma((2,)),
        ],
        compiler_params=pltpu.CompilerParams(
            collective_id=0, has_side_effects=True, vmem_limit_bytes=67043328
        ),
        name="warp",
    )(surf_xyz, surf_disp, neighbours, vol_xyz)


def solution(mesh):
    spec = P(None, ("blk", "wide"))
    return jax.shard_map(
        on_device, mesh=mesh, in_specs=(spec,) * 4, out_specs=spec, check_vma=False
    )
```
